32 devices in a mesh: dp: 8 (over y, x, core), mp: 4 (over z).
Axes of the slice: x: 2, y: 2, z: 4, core: 2. Of those that a mesh axis runs over, the one named last changes fastest.
Arguments:
- factor_rows: bfloat16 [4, 8, 8, 768], P('mp', None, 'dp')
- old_statistic: float32 [8, 4, 768, 768], P('dp', 'mp'), may hold values from -1 to 2, as said below
- assignment: int32 [4, 8], P('mp'), may hold values from 0 to 7, each once within a row
- gradient: bfloat16 [8, 4, 768, 512], P('dp', None, None, 'mp'), may hold values from -3 to 3
Outputs:
- update: bfloat16 [8, 4, 768, 512], P('dp', None, None, 'mp')
The draws below stay inside these ranges and needn't reach their ends.
Inputs may be any that keep to these rules, and one draw needn't show every extreme that they name: Each row of assignment names every block number once. `old_statistic`: each block is symmetric positive definite.
All inputs are finite; a program needn't handle non-finite values.
Results may differ from the reference program's by a relative error of at most 0.001.
The reference program's roundings to bfloat16 on the way count: a program that leaves them out, or rounds other values in their place, can miss the bound.
Values may be sent and summed in bfloat16 or wider, within the bound.
No kernel may reach another device: no remote copies, remote signals or barrier semaphores. Data moves between devices by JAX's collectives and lax.ppermute only.
A program may use at most 64 MiB of HBM per device.

```python
import math
import jax
import jax.numpy as jnp
from jax import lax

B = 768
COLS = 512
ROWS = 1
N_DP = 8
N_MP = 4


def draw_factor_rows(key, part):
    count = N_DP * ROWS
    shape = (N_MP, N_DP, count, B)
    key_base, key_scale = jax.random.split(jax.random.fold_in(key, 11), 2)
    base = jnp.clip(jax.random.normal(key_base, shape, jnp.float32), -6.0, 6.0)
    energy = jnp.exp(jax.random.uniform(key_scale, shape[:3] + (1,), jnp.float32, math.log(0.003), math.log(0.3)))
    scales = jnp.sqrt(energy * (count / B))
    return (base * scales).astype(jnp.bfloat16)


def draw_old_statistic(key, part):
    shape = (N_DP, N_MP, B, B)
    key_noise, key_diag = jax.random.split(jax.random.fold_in(key, 23))
    noise = jnp.clip(jax.random.normal(key_noise, shape, jnp.float32), -6.0, 6.0)
    noise = noise * (0.5 / math.sqrt(B))
    symmetric = 0.5 * (noise + jnp.swapaxes(noise, 2, 3))
    whole = jnp.eye(B, dtype=jnp.float32) + symmetric
    diagonal = 1.0 / jax.random.uniform(key_diag, shape[:3], jnp.float32, 1.0, float(B))
    roots = jnp.sqrt(diagonal)
    outer = roots[..., :, None] * roots[..., None, :]
    result = outer * whole
    return result


def shard_levels(stream_key, dims, pieces, least, high):
    level, own = 1.0, jax.random.fold_in(stream_key, 6)
    for dim, parts in pieces:
        steps = jnp.exp(jax.random.uniform(jax.random.fold_in(own, dim), (parts,), jnp.float32, least / len(pieces), high / len(pieces)))
        level = level * jnp.repeat(steps, dims[dim] // parts).reshape([-1 if axis == dim else 1 for axis in range(len(dims))])
    return level


def centred(stream_key, shape, deviation, reach, cuts=(), kind=jnp.bfloat16):
    factor_of = shard_levels(stream_key, shape, cuts, -0.22, 0.18) if cuts else 1.0
    values = jax.random.normal(stream_key, shape, jnp.float32) * deviation * factor_of
    return jnp.minimum(jnp.maximum(values, -reach), reach).astype(kind)


def setup_inputs(seed: int = 0) -> dict:
    key_list = jax.random.split(jax.random.key(seed), 5)
    factor_rows = draw_factor_rows(jax.random.fold_in(key_list[4], 71), 0)
    old_statistic = draw_old_statistic(jax.random.fold_in(key_list[4], 71), 0)
    assignment = jax.vmap(lambda own: jax.random.permutation(own, N_DP))(jax.random.split(key_list[2], N_MP)).reshape((N_MP, N_DP)).astype(jnp.int32)
    gradient = centred(key_list[3], (N_DP, N_MP, B, COLS), 0.5, 3.0, ((0, 8), (3, 4)))
    return {"factor_rows": factor_rows, "old_statistic": old_statistic, "assignment": assignment, "gradient": gradient}


def newton_factors(statistic):
    identity = jnp.eye(statistic.shape[0], dtype=jnp.float32)
    frob_norm = jnp.sqrt(jnp.sum(statistic * statistic) + 1e-06)
    normed = statistic / frob_norm
    step_one = ((5.0 * identity - normed) * 0.25).astype(jnp.bfloat16)
    square_one = jnp.dot(step_one, step_one, preferred_element_type=jnp.float32).astype(jnp.bfloat16)
    product_one = jnp.dot(square_one, normed.astype(jnp.bfloat16), preferred_element_type=jnp.float32).astype(jnp.bfloat16)
    coupled_one = jnp.dot(square_one, product_one, preferred_element_type=jnp.float32)
    step_two = ((5.0 * identity - coupled_one) * 0.25).astype(jnp.bfloat16)
    square_two = jnp.dot(step_two, step_two, preferred_element_type=jnp.float32).astype(jnp.bfloat16)
    product_two = jnp.dot(square_two, coupled_one.astype(jnp.bfloat16), preferred_element_type=jnp.float32).astype(jnp.bfloat16)
    coupled_two = jnp.dot(square_two, product_two, preferred_element_type=jnp.float32)
    step_three = ((5.0 * identity - coupled_two) / (4.0 * jnp.sqrt(jnp.sqrt(frob_norm)))).astype(jnp.bfloat16)
    return (step_one, step_two, step_three)

def apply_factors(step_one, step_two, step_three, block):
    first_pass = jnp.dot(step_three, block, preferred_element_type=jnp.float32).astype(jnp.bfloat16)
    second_pass = jnp.dot(step_two, first_pass, preferred_element_type=jnp.float32).astype(jnp.bfloat16)
    return jnp.dot(step_one, second_pass, preferred_element_type=jnp.float32).astype(jnp.bfloat16)

def reference(factor_rows, old_statistic, assignment, gradient):
    count = factor_rows.shape[2]

    def refresh_block(flat_index):
        owner_dp = flat_index // N_MP
        owner_mp = flat_index % N_MP
        block_id = assignment[owner_mp, owner_dp]
        factors = factor_rows[owner_mp, block_id]
        gram = lax.dot_general(factors, factors, (((0,), (0,)), ((), ())), preferred_element_type=jnp.float32)
        statistic = old_statistic[owner_dp, owner_mp] + gram / count
        step_one, step_two, step_three = newton_factors(statistic)
        return apply_factors(step_one, step_two, step_three, gradient[owner_dp, owner_mp])
    updated = lax.map(refresh_block, jnp.arange(N_DP * N_MP, dtype=jnp.int32))
    return updated.reshape(N_DP, N_MP, B, COLS)
```

```python
import functools

import jax
import jax.numpy as jnp
from jax import lax
from jax.experimental import pallas as pl
from jax.experimental.pallas import tpu as pltpu
from jax.sharding import PartitionSpec as P

F32 = jnp.float32
BF16 = jnp.bfloat16
VMEM = pl.BlockSpec(memory_space=pltpu.VMEM)
SMEM = pl.BlockSpec(memory_space=pltpu.SMEM)


def dot(a, b):
    return jnp.dot(a, b, preferred_element_type=F32)


def pick_kernel(assignment, rows, out):
    for owner in range(out.shape[0]):
        out[owner] = rows[assignment[0, owner]].astype(out.dtype)


def pick(factor_rows, assignment):
    blocks, rows, width = factor_rows.shape
    return pl.pallas_call(
        pick_kernel,
        out_shape=jax.ShapeDtypeStruct((blocks, rows, width), F32),
        in_specs=[SMEM, VMEM],
        out_specs=VMEM,
        name="pick",
    )(assignment, factor_rows)


def newton_kernel(block, rows_ref, old, s1, s2, s3, stat, normed, square, product, coupled):
    order = old.shape[0]
    rows = rows_ref[...].reshape(rows_ref.shape[0], order).astype(BF16)
    strips = [slice(start, start + block) for start in range(0, order, block)]

    def five_eye(strip):
        shape = (block, order)
        row = lax.broadcasted_iota(jnp.int32, shape, 0) + strip.start
        column = lax.broadcasted_iota(jnp.int32, shape, 1)
        return jnp.where(row == column, F32(5.0), F32(0.0))

    total = jnp.zeros((1, order), F32)
    for strip in strips:
        gram = lax.dot_general(
            rows[:, strip], rows, (((0,), (0,)), ((), ())), preferred_element_type=F32
        )
        value = old[strip, :] + gram / rows.shape[0]
        stat[strip, :] = value
        total = total + jnp.sum(value * value, axis=0, keepdims=True)
    frob = jnp.sqrt(jnp.sum(total, axis=1, keepdims=True) + F32(1e-06))
    inverse = 1.0 / frob
    for strip in strips:
        value = stat[strip, :] * inverse
        normed[strip, :] = value.astype(BF16)
        s1[strip, :] = ((five_eye(strip) - value) * 0.25).astype(BF16)

    def multiply(step, state):
        for strip in strips:
            square[strip, :] = dot(step[strip, :], step[...]).astype(BF16)
        for strip in strips:
            product[strip, :] = dot(square[strip, :], state[...]).astype(BF16)

    multiply(s1, normed)
    for strip in strips:
        value = dot(square[strip, :], product[...])
        coupled[strip, :] = value.astype(BF16)
        s2[strip, :] = ((five_eye(strip) - value) * 0.25).astype(BF16)
    multiply(s2, coupled)
    scale = 1.0 / (4.0 * jnp.sqrt(jnp.sqrt(frob)))
    for strip in strips:
        value = dot(square[strip, :], product[...])
        s3[strip, :] = ((five_eye(strip) - value) * scale).astype(BF16)


def newton(rows, old):
    order = old.shape[-1]
    block = 256 if order % 256 == 0 else order
    factor = jax.ShapeDtypeStruct((order, order), BF16)
    return pl.pallas_call(
        functools.partial(newton_kernel, block),
        out_shape=[factor] * 3,
        in_specs=[VMEM, VMEM],
        out_specs=[VMEM] * 3,
        scratch_shapes=[pltpu.VMEM((order, order), F32)] + [pltpu.VMEM((order, order), BF16)] * 4,
        compiler_params=pltpu.CompilerParams(vmem_limit_bytes=24 << 20),
        cost_estimate=pl.CostEstimate(
            flops=12 * order**3, bytes_accessed=10 * order * order, transcendentals=0
        ),
        name="newton",
    )(rows, old)


def apply_kernel(s1, s2, s3, *refs):
    half = len(refs) // 2
    value = jnp.concatenate([ref[...] for ref in refs[:half]], axis=1)
    for step in (s3, s2, s1):
        value = dot(step[...], value).astype(BF16)
    width = value.shape[1] // half
    for index in range(half):
        refs[half + index][...] = value[:, index * width : (index + 1) * width]


def apply(factors, *blocks):
    order, width = blocks[0].shape
    return pl.pallas_call(
        apply_kernel,
        out_shape=[jax.ShapeDtypeStruct((order, width), BF16)] * len(blocks),
        in_specs=[VMEM] * (3 + len(blocks)),
        out_specs=[VMEM] * len(blocks),
        compiler_params=pltpu.CompilerParams(vmem_limit_bytes=16 << 20),
        cost_estimate=pl.CostEstimate(
            flops=6 * order * order * width * len(blocks),
            bytes_accessed=6 * order * order,
            transcendentals=0,
        ),
        name="apply",
    )(*factors, *blocks)


def solution(mesh):
    n_mp = mesh.shape["mp"]

    def exchange(block, flip):
        return lax.ppermute(block, "mp", [(i, i ^ flip) for i in range(n_mp)])

    def body(factor_rows, old_statistic, assignment, gradient):
        me = lax.axis_index("mp")
        blocks = gradient[0]

        def mine(flip):
            return lax.dynamic_index_in_dim(blocks, me ^ flip, 0, keepdims=False)

        picked = pick(factor_rows[0], assignment)
        arrived = lax.all_to_all(picked, "dp", split_axis=0, concat_axis=0, tiled=True)
        rows = arrived.reshape(-1, arrived.shape[-1])
        flips = list(range(n_mp - 1, 0, -1))
        came = {flip: exchange(mine(flip), flip) for flip in flips}
        factors = newton(rows, old_statistic[0, 0])
        own, first = apply(factors, mine(0), came[flips[0]])
        done = {0: own, flips[0]: exchange(first, flips[0])}
        for flip in flips[1:]:
            done[flip] = exchange(apply(factors, came[flip])[0], flip)
        result = jnp.zeros_like(blocks)
        for flip, value in done.items():
            result = lax.dynamic_update_index_in_dim(result, value, me ^ flip, 0)
        return result[None]

    return jax.shard_map(
        body,
        mesh=mesh,
        in_specs=(
            P("mp", None, "dp", None),
            P("dp", "mp", None, None),
            P("mp", None),
            P("dp", None, None, "mp"),
        ),
        out_specs=P("dp", None, None, "mp"),
        check_vma=False,
    )
```

```python
import functools

import jax
import jax.numpy as jnp
from jax import lax
from jax.experimental import pallas as pl
from jax.experimental.pallas import tpu as pltpu
from jax.sharding import PartitionSpec as P


F32 = jnp.float32
BF16 = jnp.bfloat16
VMEM = pl.BlockSpec(memory_space=pltpu.VMEM)
SMEM = pl.BlockSpec(memory_space=pltpu.SMEM)
HBM = pl.BlockSpec(memory_space=pltpu.HBM)


def dot(a, b):
    return jnp.dot(a, b, preferred_element_type=F32)


def pick_kernel(assignment, rows, out, wide):
    wide[...] = rows[...].astype(F32)
    for owner in range(out.shape[0]):
        out[owner] = wide[pl.ds(assignment[0, owner], 1), :]


def pick(factor_rows, assignment):
    blocks, width = factor_rows.shape
    return pl.pallas_call(
        pick_kernel,
        out_shape=jax.ShapeDtypeStruct((blocks, 1, width), F32),
        in_specs=[SMEM, VMEM],
        out_specs=VMEM,
        scratch_shapes=[pltpu.VMEM((blocks, width), F32)],
        compiler_params=pltpu.CompilerParams(vmem_limit_bytes=4 << 20),
        name="pick",
    )(assignment, factor_rows)


def load_kernel(source, out, sem):
    copy = pltpu.make_async_copy(source, out, sem)
    copy.start()
    copy.wait()


def load(array):
    return pl.pallas_call(
        load_kernel,
        out_shape=jax.ShapeDtypeStruct(array.shape, array.dtype),
        in_specs=[HBM],
        out_specs=VMEM,
        scratch_shapes=[pltpu.SemaphoreType.DMA],
        compiler_params=pltpu.CompilerParams(vmem_limit_bytes=8 << 20),
        name="load",
    )(array)


def newton_kernel(block, rows_ref, old, s1, s2, s3, stat, normed, square, product, coupled):
    order = old.shape[0]
    rows = rows_ref[...].astype(BF16)
    strips = [slice(start, start + block) for start in range(0, order, block)]

    def five_eye(strip):
        shape = (block, order)
        row = lax.broadcasted_iota(jnp.int32, shape, 0) + strip.start
        column = lax.broadcasted_iota(jnp.int32, shape, 1)
        return jnp.where(row == column, F32(5.0), F32(0.0))

    total = jnp.zeros((1, order), F32)
    for strip in strips:
        gram = lax.dot_general(
            rows[:, strip], rows, (((0,), (0,)), ((), ())), preferred_element_type=F32
        )
        value = old[strip, :] + gram / rows.shape[0]
        stat[strip, :] = value
        total = total + jnp.sum(value * value, axis=0, keepdims=True)
    frob = jnp.sqrt(jnp.sum(total, axis=1, keepdims=True) + F32(1e-06))
    inverse = 1.0 / frob
    for strip in strips:
        value = stat[strip, :] * inverse
        normed[strip, :] = value.astype(BF16)
        s1[strip, :] = ((five_eye(strip) - value) * 0.25).astype(BF16)

    def multiply(step, state):
        for strip in strips:
            square[strip, :] = dot(step[strip, :], step[...]).astype(BF16)
        for strip in strips:
            product[strip, :] = dot(square[strip, :], state[...]).astype(BF16)

    multiply(s1, normed)
    for strip in strips:
        value = dot(square[strip, :], product[...])
        coupled[strip, :] = value.astype(BF16)
        s2[strip, :] = ((five_eye(strip) - value) * 0.25).astype(BF16)
    multiply(s2, coupled)
    scale = 1.0 / (4.0 * jnp.sqrt(jnp.sqrt(frob)))
    for strip in strips:
        value = dot(square[strip, :], product[...])
        s3[strip, :] = ((five_eye(strip) - value) * scale).astype(BF16)


def newton(rows, old):
    order = old.shape[-1]
    block = 256 if order % 256 == 0 else order
    factor = jax.ShapeDtypeStruct((order, order), BF16)
    return pl.pallas_call(
        functools.partial(newton_kernel, block),
        out_shape=[factor] * 3,
        in_specs=[VMEM, VMEM],
        out_specs=[VMEM] * 3,
        scratch_shapes=[pltpu.VMEM((order, order), F32)] + [pltpu.VMEM((order, order), BF16)] * 4,
        compiler_params=pltpu.CompilerParams(vmem_limit_bytes=24 << 20),
        cost_estimate=pl.CostEstimate(
            flops=12 * order**3, bytes_accessed=10 * order * order, transcendentals=0
        ),
        name="newton",
    )(rows, old)


def apply_kernel(s1, s2, s3, *refs):
    half = len(refs) // 2
    value = jnp.concatenate([ref[...] for ref in refs[:half]], axis=1)
    for step in (s3, s2, s1):
        value = dot(step[...], value).astype(BF16)
    width = value.shape[1] // half
    for index in range(half):
        refs[half + index][...] = value[:, index * width : (index + 1) * width]


def apply(factors, *blocks):
    order, width = blocks[0].shape
    return pl.pallas_call(
        apply_kernel,
        out_shape=[jax.ShapeDtypeStruct((order, width), BF16)] * len(blocks),
        in_specs=[VMEM] * (3 + len(blocks)),
        out_specs=[VMEM] * len(blocks),
        compiler_params=pltpu.CompilerParams(vmem_limit_bytes=16 << 20),
        cost_estimate=pl.CostEstimate(
            flops=6 * order * order * width * len(blocks),
            bytes_accessed=6 * order * order,
            transcendentals=0,
        ),
        name="apply",
    )(*factors, *blocks)


def solution(mesh):
    n_mp = mesh.shape["mp"]
    flips = list(range(n_mp - 1, 0, -1))

    def exchange(block, flip):
        return lax.ppermute(block, "mp", [(i, i ^ flip) for i in range(n_mp)])

    def body(factor_rows, old_statistic, assignment, gradient):
        me = lax.axis_index("mp")
        blocks = gradient[0]

        def mine(flip):
            return lax.dynamic_index_in_dim(blocks, me ^ flip, 0, keepdims=False)

        came = {flip: exchange(mine(flip), flip) for flip in flips}
        picked = pick(factor_rows[0, :, 0], assignment)
        arrived = lax.all_to_all(picked, "dp", split_axis=0, concat_axis=0, tiled=True)
        rows = arrived.reshape(-1, arrived.shape[-1])
        old = load(old_statistic[0, 0])
        factors = newton(rows, old)
        own, first = apply(factors, mine(0), came[flips[0]])
        done = {0: own, flips[0]: exchange(first, flips[0])}
        for flip in flips[1:]:
            done[flip] = exchange(apply(factors, came[flip])[0], flip)
        result = jnp.zeros_like(blocks)
        for flip, value in done.items():
            result = lax.dynamic_update_index_in_dim(result, value, me ^ flip, 0)
        return result[None]

    return jax.shard_map(
        body,
        mesh=mesh,
        in_specs=(
            P("mp", None, "dp", None),
            P("dp", "mp", None, None),
            P("mp", None),
            P("dp", None, None, "mp"),
        ),
        out_specs=P("dp", None, None, "mp"),
        check_vma=False,
    )
```
